128 devices in a mesh: series: 32 (over y, z, x_hi), tm: 4 (over x_lo, core).
Axes of the slice: x: 4 (x_hi: 2, x_lo: 2; x = x_hi * 2 + x_lo), y: 4, z: 4, core: 2. Of those that a mesh axis runs over, the one named last changes fastest.
Arguments:
- observed: bfloat16 [524288, 2048], P('series', 'tm'), may hold values from -6 to 6
- flags: int32 [524288, 16], P('series', 'tm'), may hold values 0 or 1
- factors: bfloat16 [524288, 64], P('series'), may hold values from -0.75 to 0.75
- basis: float32 [64, 2048], P(None, 'tm'), may hold values from -6 to 6
- tcn_weights: float32 [4, 64, 64], replicated, may hold values from -0.5 to 0.5
- tcn_bias: float32 [2, 64], replicated, may hold values from -3 to 3
- dilations: int32 [2], replicated, may hold values from 1 to 64, as said below
Outputs:
- new_basis: float32 [64, 2048], P(None, 'tm')
- new_factors: bfloat16 [524288, 64], P('series')
The draws below stay inside these ranges and needn't reach their ends.
Inputs may be any that keep to these rules, and one draw needn't show every extreme that they name: `dilations`: each dilation is between 1 and 64, and at least one of the two equals 64.
All inputs are finite; a program needn't handle non-finite values. No bound on the sum of `flags` on one device may be relied on, other than what follows from the above.
Results may differ from the reference program's by a relative error of at most 0.002.
The reference program's roundings to bfloat16 on the way (of `resid`) count: a program that leaves them out, or rounds other values in their place, can miss the bound.
Values may be sent and summed in bfloat16 or wider, within the bound.
A program may use at most 192 MiB of HBM per device.

```python
import math
import jax
import jax.numpy as jnp
from jax import lax

K = 64
R_DEV = 16384
DMAX = 64
BLK = 128
ITERS = 3
HALO = 129
NSERIES = 524288
TT = 2048


def draw_dilations(key, part):
    first_key = jax.random.fold_in(key, 11)
    order_key = jax.random.fold_in(key, 12)
    other = jax.random.randint(first_key, (1,), 1, DMAX + 1).astype(jnp.int32)
    both = jnp.concatenate([other, jnp.full((1,), DMAX, jnp.int32)])
    order = jax.random.permutation(order_key, 2)
    return both[order].astype(jnp.int32)


def draw_factors(key, part):
    base_key = jax.random.fold_in(key, 21)
    shared_key = jax.random.fold_in(key, 22)
    level_key = jax.random.fold_in(key, 23)
    blocks = NSERIES // R_DEV
    base = jax.random.normal(base_key, (NSERIES, K), jnp.float32)
    shared = jax.random.normal(shared_key, (NSERIES, 1), jnp.float32)
    levels = jnp.exp(jax.random.uniform(level_key, (blocks, K), jnp.float32, -0.7, 0.7))
    column_scale = jnp.repeat(levels, R_DEV, axis=0)
    values = 0.15 * shared + base * column_scale * (1.0 / math.sqrt(K))
    return jnp.clip(values, -0.75, 0.75).astype(jnp.bfloat16)


def set_ends(array, own_key, smallest, high):
    place = [jax.random.randint(jax.random.fold_in(own_key, axis), (), 0, length) for axis, length in enumerate(array.shape)]
    longest = array.shape.index(max(array.shape))
    neighbour = place[:longest] + [(place[longest] + 1) % array.shape[longest]] + place[longest + 1:]
    return array.at[tuple(place)].set(smallest).at[tuple(neighbour)].set(high)


def steps_of(own_key, dims, pieces, smallest, top_value):
    def one(dim, parts):
        heights = jax.random.uniform(jax.random.fold_in(jax.random.fold_in(own_key, 6), dim), (parts,), jnp.float32, smallest / len(pieces), top_value / len(pieces))
        return jnp.repeat(jnp.exp(heights), dims[dim] // parts).reshape((-1,) + (1,) * (len(dims) - dim - 1))

    level = one(*pieces[0])
    for cut in pieces[1:]:
        level = level * one(*cut)
    return level


def centred(own_key, shape, spread, most, cuts=(), held_as=jnp.bfloat16):
    factor_of = steps_of(own_key, shape, cuts, -0.22, 0.18) if cuts else 1.0
    array = jax.random.normal(own_key, shape, jnp.float32) * spread * factor_of
    return jnp.minimum(jnp.maximum(array, -most), most).astype(held_as)


def setup_inputs(seed: int = 0) -> dict:
    arg_keys = jax.random.split(jax.random.key(seed), 8)
    observed = centred(arg_keys[0], (NSERIES, TT), 1.0, 6.0, ((0, 32), (1, 4)))
    flags = set_ends((jax.random.randint(arg_keys[1], (NSERIES, TT // BLK), 0, 4) < 3).astype(jnp.int32), jax.random.fold_in(arg_keys[1], 1), 0, 1)
    factors = draw_factors(jax.random.fold_in(arg_keys[7], 71), 0)
    basis = centred(arg_keys[3], (K, TT), 1.0, 6.0, ((1, 4),), jnp.float32)
    tcn_weights = centred(arg_keys[4], (4, K, K), (2 * K) ** -0.5, 0.5, (), jnp.float32)
    tcn_bias = centred(arg_keys[5], (2, K), 0.5, 3.0, (), jnp.float32)
    dilations = draw_dilations(jax.random.fold_in(arg_keys[7], 71), 0)
    return dict(observed=observed, flags=flags, factors=factors, basis=basis, tcn_weights=tcn_weights, tcn_bias=tcn_bias, dilations=dilations)


def delay(field, steps):
    padded = jnp.pad(field, ((0, 0), (DMAX, 0)))
    return lax.dynamic_slice_in_dim(padded, (DMAX - steps).astype(jnp.int32), field.shape[1], 1)

def mix(weight, field):
    return jnp.dot(weight, field, precision=lax.Precision.HIGHEST)

def tcn_error(padded, tcn_weights, tcn_bias, dilations, keep):
    shifted = delay(padded, jnp.int32(1))
    hidden = jax.nn.relu(mix(tcn_weights[0], delay(shifted, dilations[0])) + mix(tcn_weights[1], shifted) + tcn_bias[0][:, None])
    output = mix(tcn_weights[2], delay(hidden, dilations[1])) + mix(tcn_weights[3], hidden) + tcn_bias[1][:, None]
    return (padded - shifted - output)[:, -keep:]

def resid_block(fac, obs, flg, basis_b):
    pred = jnp.dot(fac, basis_b, preferred_element_type=jnp.float32)
    diff = (pred - obs.astype(jnp.float32)).reshape(fac.shape[0], -1, BLK) * flg[:, :, None].astype(jnp.float32)
    return diff.reshape(fac.shape[0], -1).astype(jnp.bfloat16)

def reference(observed, flags, factors, basis, tcn_weights, tcn_bias, dilations):
    blocks = NSERIES // R_DEV
    fac_b = factors.reshape(blocks, R_DEV, K)
    obs_b = observed.reshape(blocks, R_DEV, TT)
    flg_b = flags.reshape(blocks, R_DEV, TT // BLK)
    current = basis
    for step in range(ITERS):
        basis_b = current.astype(jnp.bfloat16)

        def accumulate(total, item):
            fac, obs, flg = item
            resid = resid_block(fac, obs, flg, basis_b)
            return (total + lax.dot_general(fac, resid, (((0,), (0,)), ((), ())), preferred_element_type=jnp.float32), None)
        data_grad, unused = lax.scan(accumulate, jnp.zeros((K, TT), jnp.float32), (fac_b, obs_b, flg_b))
        padded = jnp.pad(current, ((0, 0), (HALO, 0)))
        error, pull = jax.vjp(lambda v: tcn_error(v, tcn_weights, tcn_bias, dilations, TT), padded)
        reg_grad = pull(0.1 * error)[0][:, HALO:]
        grad = data_grad * (1.0 / jnp.sqrt(jnp.float32(NSERIES))) + reg_grad
        norm = jnp.sqrt(jnp.mean(grad * grad) + 1e-06)
        current = current - 0.1 * grad / norm
    basis_b = current.astype(jnp.bfloat16)
    coef = 0.1 / jnp.sqrt(jnp.float32(TT))

    def update(item):
        fac, obs, flg = item
        resid = resid_block(fac, obs, flg, basis_b)
        fgrad = lax.dot_general(resid, basis_b, (((1,), (1,)), ((), ())), preferred_element_type=jnp.float32)
        return (fac.astype(jnp.float32) - coef * fgrad).astype(jnp.bfloat16)
    new_factors = lax.map(update, (fac_b, obs_b, flg_b)).reshape(NSERIES, K)
    return (current, new_factors)
```

```python
import functools
import math

import jax
import jax.numpy as jnp
from jax import lax
from jax.experimental import pallas as pl
from jax.experimental.pallas import tpu as pltpu
from jax.sharding import PartitionSpec as P

K = 64
BLK = 128
ITERS = 3
S1 = 2048
W1 = 3
S4 = 1024
W4 = 3
LAG = 2
F32 = jnp.float32
BF16 = jnp.bfloat16
MESH = pl.DeviceIdType.MESH
ANY = pl.BlockSpec(memory_space=pl.ANY)
VMEM = pl.BlockSpec(memory_space=pltpu.VMEM)
SMEM = pl.BlockSpec(memory_space=pltpu.SMEM)
DMA = pltpu.SemaphoreType.DMA
CONTRACT_LAST = (((1,), (1,)), ((), ()))
CONTRACT_FIRST = (((0,), (0,)), ((), ()))


def dot(a, b, dims=(((1,), (0,)), ((), ()))):
    return lax.dot_general(a, b, dims, preferred_element_type=F32)


def gram_kernel(flg, ft, obs, out, ov, fv, mv, c_acc, g_acc, so, sf, sm):
    n = obs.shape[0] // S1

    def copies(i):
        sl = pl.ds(i * S1, S1)
        return (
            pltpu.make_async_copy(ft.at[:, sl], fv.at[:, sl], sf.at[i]),
            pltpu.make_async_copy(flg.at[:, sl], mv.at[:, sl], sm.at[i]),
            pltpu.make_async_copy(obs.at[sl], ov.at[sl], so.at[i]),
        )

    for i in range(W1):
        for c in copies(i):
            c.start()
    c_acc[...] = jnp.zeros_like(c_acc)
    g_acc[...] = jnp.zeros_like(g_acc)
    for i in range(n):
        for c in copies(i):
            c.wait()
        if i + W1 < n:
            for c in copies(i + W1):
                c.start()
        sl = pl.ds(i * S1, S1)
        f = fv[:, sl]
        m = mv[:, sl].astype(F32).astype(BF16)
        masked = jnp.concatenate([f * m[b : b + 1, :] for b in range(4)], axis=0)
        g_acc[...] += dot(masked, f, CONTRACT_LAST)
        c_acc[0:128] += dot(masked[0:128], ov[sl, 0:256])
        c_acc[128:256] += dot(masked[128:256], ov[sl, 256:512])
    for b in range(4):
        out[b * K : b * K + K] = c_acc[b * K : b * K + K, (b % 2) * BLK : (b % 2) * BLK + BLK]
    for h in range(2):
        out[256 + K * h : 320 + K * h] = jnp.concatenate(
            [g_acc[128 * h : 128 * h + K], g_acc[128 * h + K : 128 * h + 128]], axis=1
        )


def gram(flags_t, factors_t, observed):
    rows = observed.shape[0]
    n = rows // S1
    return pl.pallas_call(
        gram_kernel,
        in_specs=[ANY] * 3,
        out_specs=VMEM,
        out_shape=jax.ShapeDtypeStruct((384, 128), F32),
        scratch_shapes=[
            pltpu.VMEM((rows, 512), BF16),
            pltpu.VMEM((K, rows), BF16),
            pltpu.VMEM((4, rows), jnp.int32),
            pltpu.VMEM((256, 256), F32),
            pltpu.VMEM((256, K), F32),
            DMA((n,)),
            DMA((n,)),
            DMA((n,)),
        ],
        name="gram",
    )(flags_t, factors_t, observed)


def reduce_kernel(
    q, basis, full, xall, ry, az, rz, bx, rx, ssem, ysem, zsem, xsem, gzsem, gysem, wsem, bsem
):
    series = lax.axis_index("series")
    tm = lax.axis_index("tm")
    y, z, hi = series // 8, (series // 2) % 4, series % 2
    lo, core = tm // 2, tm % 2

    def at(yy, zz, hh, ll, cc):
        return {"series": (yy % 4) * 8 + (zz % 4) * 2 + hh % 2, "tm": (ll % 2) * 2 + cc % 2}

    peers_y = [at(y + d, z, hi, lo, core) for d in (1, 2, 3)]
    peers_z = [at(y, z + d, hi, lo, core) for d in (1, 2, 3)]
    peers_x = [at(y, z, hi + k // 2, lo + k % 2, core) for k in (1, 2, 3)]
    partner = at(y, z, hi, lo, core + 1)

    barrier = pltpu.get_barrier_semaphore()
    for p in peers_y + peers_z + peers_x + [partner]:
        pl.semaphore_signal(barrier, inc=1, device_id=p, device_id_type=MESH)
    pl.semaphore_wait(barrier, 10)

    sends = []

    def send(src, dst, sem, peer):
        c = pltpu.make_async_remote_copy(
            src, dst, ssem.at[len(sends)], sem, device_id=peer, device_id_type=MESH
        )
        c.start()
        sends.append(c)
        return c

    cy = [
        send(q.at[pl.ds(96 * ((y + d) % 4), 96)], ry.at[d - 1], ysem.at[d - 1], peers_y[d - 1])
        for d in (1, 2, 3)
    ]
    cb = send(basis, xall.at[core, lo], bsem.at[0], peers_x[0])
    xall[core, lo] = basis[...]
    for c in cy:
        c.wait_recv()
    az[...] = q[pl.ds(96 * y, 96)] + (ry[0] + ry[1] + ry[2])
    cz = [
        send(az.at[pl.ds(24 * ((z + d) % 4), 24)], rz.at[d - 1], zsem.at[d - 1], peers_z[d - 1])
        for d in (1, 2, 3)
    ]
    cb.wait_recv()
    cv = send(xall.at[core], xall.at[core], bsem.at[1], partner)
    for c in cz:
        c.wait_recv()
    part = az[pl.ds(24 * z, 24)] + (rz[0] + rz[1] + rz[2])
    bx[...] = part
    cx = [send(bx, rx.at[hi, lo], xsem.at[k - 1], peers_x[k - 1]) for k in (1, 2, 3)]
    rx[hi, lo] = part
    for c in cx:
        c.wait_recv()
    row = pl.ds(96 * y + 24 * z, 24)
    full[core, :, row, :] = rx[0] + rx[1]
    own = full.at[core, :, row, :]
    cgz = [send(own, own, gzsem.at[d - 1], peers_z[d - 1]) for d in (1, 2, 3)]
    for c in cgz:
        c.wait_recv()
    own = full.at[core, :, pl.ds(96 * y, 96), :]
    cgy = [send(own, own, gysem.at[d - 1], peers_y[d - 1]) for d in (1, 2, 3)]
    for c in cgy:
        c.wait_recv()
    cw = send(full.at[core], full.at[core], wsem, partner)
    cw.wait_recv()
    cv.wait_recv()
    for c in sends:
        c.wait_send()


def reduce_all(slab, basis):
    return pl.pallas_call(
        reduce_kernel,
        in_specs=[VMEM, VMEM],
        out_specs=[VMEM, VMEM],
        out_shape=[
            jax.ShapeDtypeStruct((2, 2, 384, 128), F32),
            jax.ShapeDtypeStruct((2, 2) + basis.shape, F32),
        ],
        scratch_shapes=[
            pltpu.VMEM((3, 96, 128), F32),
            pltpu.VMEM((96, 128), F32),
            pltpu.VMEM((3, 24, 128), F32),
            pltpu.VMEM((24, 128), F32),
            pltpu.VMEM((2, 2, 24, 128), F32),
            DMA((18,)),
            DMA((3,)),
            DMA((3,)),
            DMA((3,)),
            DMA((3,)),
            DMA((3,)),
            DMA,
            DMA((2,)),
        ],
        compiler_params=pltpu.CompilerParams(collective_id=0, has_side_effects=True),
        name="reduce_all",
    )(slab, basis)


def split(a):
    high = a.astype(BF16)
    return high, (a - high.astype(F32)).astype(BF16)


def steps_kernel(scale, dil, full, x_in, w, wt, bias, x_out):
    d0, d1 = dil[0], dil[1]
    tiles = 16
    lane = lax.broadcasted_iota(jnp.int32, (K, BLK), 1)

    def delay(v, d, before):
        rolled = [pltpu.roll(t, d, 1) for t in v]
        return [jnp.where(lane < d, before if j == 0 else rolled[j - 1], rolled[j]) for j in range(tiles)]

    def advance(v, d):
        rolled = [pltpu.roll(t, BLK - d, 1) for t in v]
        zero = jnp.zeros((K, BLK), F32)
        return [
            jnp.where(lane >= BLK - d, zero if j == tiles - 1 else rolled[j + 1], rolled[j])
            for j in range(tiles)
        ]

    def pair(weights, u, v):
        out = []
        for j in range(0, tiles, 2):
            uh, ul = split(jnp.concatenate(u[j : j + 2], axis=1))
            vh, vl = split(jnp.concatenate(v[j : j + 2], axis=1))
            r = dot(weights, jnp.concatenate([uh, vh, ul, vl], axis=0))
            r = r[0:K] + r[K : 2 * K]
            out += [r[:, 0:BLK], r[:, BLK : 2 * BLK]]
        return out

    def packed(a, b):
        ah, al = split(a)
        bh, bl = split(b)
        zero = jnp.zeros((K, 2 * K), BF16)
        top = jnp.concatenate([ah, bh, ah, bh], axis=1)
        low = jnp.concatenate([al, bl, zero], axis=1)
        return jnp.concatenate([top, low], axis=0)

    layer1, layer2 = packed(w[0], w[1]), packed(w[2], w[3])
    back1, back2 = packed(wt[0], wt[1]), packed(wt[2], wt[3])
    b0 = jnp.broadcast_to(bias[:, 0:1], (K, BLK))
    b1 = jnp.broadcast_to(bias[:, 1:2], (K, BLK))
    start = jnp.maximum(b0, 0.0)
    zero = jnp.zeros((K, BLK), F32)
    grams = []
    for j in range(tiles):
        t, b = j // 4, j % 4
        g = full[t % 2, t // 2, 256 + K * (b // 2) : 320 + K * (b // 2), K * (b % 2) : K * (b % 2) + K]
        gh, gl = split(g)
        rest = g - gh.astype(F32) - gl.astype(F32)
        grams.append(jnp.concatenate([gh, gl, rest.astype(BF16)], axis=0))
    x = [x_in[(j // 4) % 2, j // 8, :, (j % 4) * BLK : (j % 4) * BLK + BLK] for j in range(tiles)]
    for step in range(ITERS):
        z = delay(x, 1, zero)
        a = [v + b0 for v in pair(layer1, delay(z, d0, zero), z)]
        h = [jnp.maximum(v, 0.0) for v in a]
        o = pair(layer2, delay(h, d1, start), h)
        u = [0.1 * (x[j] - z[j] - o[j] - b1) for j in range(tiles)]
        dh = pair(back2, advance(u, d1), u)
        da = [jnp.where(a[j] > 0.0, dh[j], 0.0) for j in range(tiles)]
        dz = pair(back1, advance(da, d0), da)
        dx = advance([u[j] + dz[j] for j in range(tiles)], 1)
        grad = []
        total = zero
        for j in range(tiles):
            t, b = j // 4, j % 4
            r = dot(grams[j], x[j].astype(BF16))
            data = (r[0:K] + (r[K : 2 * K] + r[2 * K : 3 * K])) - full[t % 2, t // 2, b * K : b * K + K, :]
            g = data * scale + (u[j] - dx[j])
            total = total + g * g
            grad.append(g)
        norm = jnp.sqrt(jnp.sum(total, keepdims=True) * (1.0 / (K * BLK * tiles)) + 1e-06)
        x = [x[j] - 0.1 * grad[j] / norm for j in range(tiles)]
    for j in range(tiles):
        x_out[:, j * BLK : j * BLK + BLK] = x[j]


def basis_steps(scale, dilations, full, x, w, wt, bias):
    return pl.pallas_call(
        functools.partial(steps_kernel, scale),
        in_specs=[SMEM] + [VMEM] * 5,
        out_specs=VMEM,
        out_shape=jax.ShapeDtypeStruct((K, 2048), F32),
        name="basis_steps",
    )(dilations, full, x, w, wt, bias)


def factor_kernel(
    coef, flg, ft, obs, xb, out, ov, fv, mv, give, take, own, code, got, amp, gamp,
    so, sf, sm, psend, precv, csend, crecv, asend, arecv, fsend, frecv,
):
    series = lax.axis_index("series")
    tm = lax.axis_index("tm")
    lo, core = tm // 2, tm % 2
    partner = {"series": series, "tm": lo * 2 + (1 - core)}
    across = {"series": series, "tm": (1 - lo) * 2 + core}
    half = obs.shape[0] // 2
    n = half // S4

    def columns(side, i):
        return pl.ds(pl.multiple_of(side * half + i * S4, S4), S4)

    def copies(step, slot):
        side = (core + 1 + step) % 2
        sl = columns(side, step // 2)
        return (
            pltpu.make_async_copy(ft.at[:, sl], fv.at[slot], sf.at[slot]),
            pltpu.make_async_copy(flg.at[:, sl], mv.at[slot], sm.at[slot]),
            pltpu.make_async_copy(obs.at[sl], ov.at[slot], so.at[slot]),
        )

    barrier = pltpu.get_barrier_semaphore()
    for p in (partner, across):
        pl.semaphore_signal(barrier, inc=1, device_id=p, device_id_type=MESH)
    for s in range(W4):
        for c in copies(s, s):
            c.start()
    x = xb[...]
    zero = jnp.zeros((K, BLK), BF16)
    pairs = []
    for h in range(2):
        l, r = x[:, 256 * h : 256 * h + BLK], x[:, 256 * h + BLK : 256 * h + 256]
        pairs.append(
            jnp.concatenate(
                [jnp.concatenate([l, zero], axis=1), jnp.concatenate([zero, r], axis=1)], axis=0
            )
        )

    def product(step):
        slot = step % W4
        for c in copies(step, slot):
            c.wait()
        pred = dot(fv[slot], x, CONTRACT_FIRST)
        resid = (pred - ov[slot].astype(F32)).astype(BF16)
        m = mv[slot].astype(F32)
        total = None
        for h in range(2):
            r = dot(pairs[h], resid[:, 256 * h : 256 * h + 256], CONTRACT_LAST)
            t = r[0:K] * m[2 * h : 2 * h + 1] + r[K : 2 * K] * m[2 * h + 1 : 2 * h + 2]
            total = t if total is None else total + t

        return total

    def refill(step):
        @pl.when(step + W4 < 2 * n)
        def _():
            for c in copies(step + W4, step % W4):
                c.start()

    def at(ref, i):
        return ref.at[i]

    def give_copy(i):
        return pltpu.make_async_remote_copy(
            give.at[i], take.at[i], psend.at[i], precv.at[i], device_id=partner, device_id_type=MESH
        )

    def code_copy(i):
        return pltpu.make_async_remote_copy(
            code.at[i], got.at[i], csend.at[i], crecv.at[i], device_id=across, device_id_type=MESH
        )

    def amp_copy(i):
        return pltpu.make_async_remote_copy(
            amp.at[i], gamp.at[i], asend.at[i], arecv.at[i], device_id=across, device_id_type=MESH
        )

    def final_copy(i):
        sl = columns(core, i)
        return pltpu.make_async_remote_copy(
            out.at[:, sl], out.at[:, sl], fsend.at[i], frecv.at[i], device_id=partner, device_id_type=MESH
        )

    def finish(i):
        code_copy(i).wait_recv()
        amp_copy(i).wait_recv()
        mine = code[i].astype(jnp.int32).astype(F32) * amp[i]
        theirs = got[i].astype(jnp.int32).astype(F32) * gamp[i]
        old = own[i % (LAG + 1)].astype(F32)
        sl = columns(core, i)
        out[:, sl] = (old - coef * (mine + theirs)).astype(BF16)
        final_copy(i).start()

    pl.semaphore_wait(barrier, 2)

    def step(i, carry):
        give[i] = product(2 * i)
        refill(2 * i)
        give_copy(i).start()
        total = product(2 * i + 1)
        own[i % (LAG + 1)] = fv[(2 * i + 1) % W4]
        refill(2 * i + 1)
        give_copy(i).wait_recv()
        total = total + take[i]
        top = jnp.max(jnp.abs(total), axis=0, keepdims=True)
        code[i] = jnp.round(total * (32000.0 / jnp.maximum(top, 1e-30))).astype(jnp.int32).astype(jnp.int16)
        amp[i] = top * (1.0 / 32000.0)
        code_copy(i).start()
        amp_copy(i).start()

        @pl.when(i >= LAG)
        def _():
            finish(i - LAG)

        return carry

    lax.fori_loop(0, n, step, 0)
    for i in range(n - LAG, n):
        finish(i)

    def drain(i, carry):
        give_copy(i).wait_send()
        code_copy(i).wait_send()
        amp_copy(i).wait_send()
        c = final_copy(i)
        c.wait_send()
        c.wait_recv()
        return carry

    lax.fori_loop(0, n, drain, 0)


def factor_step(coef, flags_t, factors_t, observed, xb):
    rows = observed.shape[0]
    n = rows // 2 // S4
    return pl.pallas_call(
        functools.partial(factor_kernel, coef),
        in_specs=[ANY] * 3 + [VMEM],
        out_specs=VMEM,
        out_shape=jax.ShapeDtypeStruct((K, rows), BF16),
        scratch_shapes=[
            pltpu.VMEM((W4, S4, 512), BF16),
            pltpu.VMEM((W4, K, S4), BF16),
            pltpu.VMEM((W4, 4, S4), jnp.int32),
            pltpu.VMEM((n, K, S4), F32),
            pltpu.VMEM((n, K, S4), F32),
            pltpu.VMEM((LAG + 1, K, S4), BF16),
            pltpu.VMEM((n, K, S4), jnp.int16),
            pltpu.VMEM((n, K, S4), jnp.int16),
            pltpu.VMEM((n, 1, S4), F32),
            pltpu.VMEM((n, 1, S4), F32),
            DMA((W4,)),
            DMA((W4,)),
            DMA((W4,)),
        ]
        + [DMA((n,))] * 8,
        compiler_params=pltpu.CompilerParams(collective_id=1, has_side_effects=True),
        name="factor_step",
    )(flags_t, factors_t, observed, xb)


def shards(observed, flags, factors, basis, tcn_weights, tcn_bias, dilations):
    local_rows = factors.shape[0]
    local_cols = basis.shape[1]
    scale = 1.0 / math.sqrt(local_rows * lax.axis_size("series"))
    coef = 0.1 / math.sqrt(local_cols * lax.axis_size("tm"))
    flags_t, factors_t = flags.T, factors.T
    slab = gram(flags_t, factors_t, observed)
    full, whole = reduce_all(slab, basis)
    current = basis_steps(
        scale,
        dilations,
        full,
        whole,
        tcn_weights,
        jnp.swapaxes(tcn_weights, 1, 2),
        tcn_bias.T,
    )
    mine = lax.dynamic_slice_in_dim(current, lax.axis_index("tm") * local_cols, local_cols, 1)
    new_factors = factor_step(coef, flags_t, factors_t, observed, mine.astype(BF16))
    return (mine, new_factors.T)


def solution(mesh):
    return jax.shard_map(
        shards,
        mesh=mesh,
        in_specs=(
            P("series", "tm"),
            P("series", "tm"),
            P("series", None),
            P(None, "tm"),
            P(),
            P(),
            P(),
        ),
        out_specs=(P(None, "tm"), P("series", None)),
        check_vma=False,
    )
```

```python
import functools
import math

import jax
import jax.numpy as jnp
from jax import lax
from jax.experimental import pallas as pl
from jax.experimental.pallas import tpu as pltpu
from jax.sharding import PartitionSpec as P

K = 64
BLK = 128
ITERS = 3
S1 = 2048
W1 = 3
S4 = 512
LAG = 3
F32 = jnp.float32
BF16 = jnp.bfloat16
MESH = pl.DeviceIdType.MESH
ANY = pl.BlockSpec(memory_space=pl.ANY)
VMEM = pl.BlockSpec(memory_space=pltpu.VMEM)
SMEM = pl.BlockSpec(memory_space=pltpu.SMEM)
DMA = pltpu.SemaphoreType.DMA
CONTRACT_LAST = (((1,), (1,)), ((), ()))
CONTRACT_FIRST = (((0,), (0,)), ((), ()))


def dot(a, b, dims=(((1,), (0,)), ((), ()))):
    return lax.dot_general(a, b, dims, preferred_element_type=F32)


def split(a):
    high = a.astype(BF16)
    return high, (a - high.astype(F32)).astype(BF16)


def basis_steps(scale, dil, full, x_in, w, bias, x_out):
    d0, d1 = dil[0], dil[1]
    tiles = 16
    lane = lax.broadcasted_iota(jnp.int32, (K, BLK), 1)

    def delay(v, d, before):
        rolled = [pltpu.roll(t, d, 1) for t in v]
        return [jnp.where(lane < d, before if j == 0 else rolled[j - 1], rolled[j]) for j in range(tiles)]

    def advance(v, d):
        rolled = [pltpu.roll(t, BLK - d, 1) for t in v]
        zero = jnp.zeros((K, BLK), F32)
        return [
            jnp.where(lane >= BLK - d, zero if j == tiles - 1 else rolled[j + 1], rolled[j])
            for j in range(tiles)
        ]

    def pair(weights, u, v):
        out = []
        for j in range(0, tiles, 2):
            uh, ul = split(jnp.concatenate(u[j : j + 2], axis=1))
            vh, vl = split(jnp.concatenate(v[j : j + 2], axis=1))
            r = dot(weights, jnp.concatenate([uh, vh, ul, vl], axis=0))
            r = r[0:K] + r[K : 2 * K]
            out += [r[:, 0:BLK], r[:, BLK : 2 * BLK]]
        return out

    def packed(a, b):
        ah, al = split(a)
        bh, bl = split(b)
        zero = jnp.zeros((K, 2 * K), BF16)
        top = jnp.concatenate([ah, bh, ah, bh], axis=1)
        low = jnp.concatenate([al, bl, zero], axis=1)
        return jnp.concatenate([top, low], axis=0)

    layer1, layer2 = packed(w[0], w[1]), packed(w[2], w[3])
    back1, back2 = packed(w[0].T, w[1].T), packed(w[2].T, w[3].T)
    eye = lax.broadcasted_iota(jnp.int32, (K, K), 0) == lax.broadcasted_iota(jnp.int32, (K, K), 1)

    def column(i):
        c = jnp.sum(jnp.where(eye, bias[i : i + 1, :], 0.0), axis=1, keepdims=True)
        return jnp.broadcast_to(c, (K, BLK))

    b0, b1 = column(0), column(1)
    start = jnp.maximum(b0, 0.0)
    zero = jnp.zeros((K, BLK), F32)
    grams = []
    for j in range(tiles):
        t, b = j // 4, j % 4
        g = full[t % 2, t // 2, 256 + K * (b // 2) : 320 + K * (b // 2), K * (b % 2) : K * (b % 2) + K]
        gh, gl = split(g)
        rest = g - gh.astype(F32) - gl.astype(F32)
        grams.append(jnp.concatenate([gh, gl, rest.astype(BF16)], axis=0))
    x = [x_in[(j // 4) % 2, j // 8, :, (j % 4) * BLK : (j % 4) * BLK + BLK] for j in range(tiles)]
    for step in range(ITERS):
        z = delay(x, 1, zero)
        a = [v + b0 for v in pair(layer1, delay(z, d0, zero), z)]
        h = [jnp.maximum(v, 0.0) for v in a]
        o = pair(layer2, delay(h, d1, start), h)
        u = [0.1 * (x[j] - z[j] - o[j] - b1) for j in range(tiles)]
        dh = pair(back2, advance(u, d1), u)
        da = [jnp.where(a[j] > 0.0, dh[j], 0.0) for j in range(tiles)]
        dz = pair(back1, advance(da, d0), da)
        dx = advance([u[j] + dz[j] for j in range(tiles)], 1)
        grad = []
        total = zero
        for j in range(tiles):
            t, b = j // 4, j % 4
            r = dot(grams[j], x[j].astype(BF16))
            data = (r[0:K] + (r[K : 2 * K] + r[2 * K : 3 * K])) - full[t % 2, t // 2, b * K : b * K + K, :]
            g = data * scale + (u[j] - dx[j])
            total = total + g * g
            grad.append(g)
        norm = jnp.sqrt(jnp.sum(total, keepdims=True) * (1.0 / (K * BLK * tiles)) + 1e-06)
        x = [x[j] - 0.1 * grad[j] / norm for j in range(tiles)]
    for j in range(tiles):
        x_out[j // 4, :, (j % 4) * BLK : (j % 4) * BLK + BLK] = x[j]


def kernel(
    scale, coef, dil, w, bias, basis, flg, ft, obs, new_basis, out,
    ov, fv, mv, c_acc, g_acc, q, ryz, bx, rx, full, xall, xs, give, take, code, got, amp, gamp,
    so, sf, sm, ssem, yzsem, xsem, gsem, wsem, bsem,
    psend, precv, csend, crecv, asend, arecv, fsend, frecv,
):
    series = lax.axis_index("series")
    tm = lax.axis_index("tm")
    y, z, hi = series // 8, (series // 2) % 4, series % 2
    lo, core = tm // 2, tm % 2

    def at(yy, zz, hh, ll, cc):
        return {"series": (yy % 4) * 8 + (zz % 4) * 2 + hh % 2, "tm": (ll % 2) * 2 + cc % 2}

    order = sorted(range(1, 16), key=lambda k: (min(k // 4, 4 - k // 4) + min(k % 4, 4 - k % 4), k))
    peers = {k: at(y + k // 4, z + k % 4, hi, lo, core) for k in order}
    peers_x = [at(y, z, hi + k // 2, lo + k % 2, core) for k in (1, 2, 3)]
    across = peers_x[0]
    partner = at(y, z, hi, lo, core + 1)

    barrier = pltpu.get_barrier_semaphore()
    for p in [*peers.values(), *peers_x, partner]:
        pl.semaphore_signal(barrier, inc=1, device_id=p, device_id_type=MESH)

    sends = []

    def send(src, dst, sem, peer):
        c = pltpu.make_async_remote_copy(
            src, dst, ssem.at[len(sends)], sem, device_id=peer, device_id_type=MESH
        )
        c.start()
        sends.append(c)
        return c

    n = obs.shape[0] // S1

    def copies(i):
        sl = pl.ds(i * S1, S1)
        return (
            pltpu.make_async_copy(ft.at[:, sl], fv.at[:, sl], sf.at[i]),
            pltpu.make_async_copy(flg.at[:, sl], mv.at[:, sl], sm.at[i]),
            pltpu.make_async_copy(obs.at[sl], ov.at[sl], so.at[i]),
        )

    for i in range(W1):
        for c in copies(i):
            c.start()
    xall[core, lo] = basis[...]
    c_acc[...] = jnp.zeros_like(c_acc)
    g_acc[...] = jnp.zeros_like(g_acc)
    for i in range(n):
        for c in copies(i):
            c.wait()
        if i + W1 < n:
            for c in copies(i + W1):
                c.start()
        sl = pl.ds(i * S1, S1)
        f = fv[:, sl]
        m = mv[:, sl].astype(F32).astype(BF16)
        masked = jnp.concatenate([f * m[b : b + 1, :] for b in range(4)], axis=0)
        g_acc[...] += dot(masked, f, CONTRACT_LAST)
        c_acc[0:128] += dot(masked[0:128], ov[sl, 0:256])
        c_acc[128:256] += dot(masked[128:256], ov[sl, 256:512])
        if i == 3:
            pl.semaphore_wait(barrier, 19)
            cb = send(basis, xall.at[core, lo], bsem.at[0], across)
    for b in range(4):
        q[b * K : b * K + K] = c_acc[b * K : b * K + K, (b % 2) * BLK : (b % 2) * BLK + BLK]
    for h in range(2):
        q[256 + K * h : 320 + K * h] = jnp.concatenate(
            [g_acc[128 * h : 128 * h + K], g_acc[128 * h + K : 128 * h + 128]], axis=1
        )

    def rows(dy, dz):
        return pl.ds(96 * ((y + dy) % 4) + 24 * ((z + dz) % 4), 24)

    cq = [send(q.at[rows(k // 4, k % 4)], ryz.at[k - 1], yzsem.at[k - 1], peers[k]) for k in reversed(order)]
    cb.wait_recv()
    cv = send(xall.at[core], xall.at[core], bsem.at[1], partner)
    for c in cq:
        c.wait_recv()
    v = [q[rows(0, 0)]] + [ryz[k] for k in range(15)]
    while len(v) > 1:
        v = [v[k] + v[k + 1] for k in range(0, len(v), 2)]
    bx[...] = v[0]
    cx = [send(bx, rx.at[hi, lo], xsem.at[k - 1], peers_x[k - 1]) for k in (1, 2, 3)]
    rx[hi, lo] = v[0]
    for c in cx:
        c.wait_recv()
    row = rows(0, 0)
    full[core, :, row, :] = rx[0] + rx[1]
    own = full.at[core, :, row, :]
    cg = {k: send(own, own, gsem.at[k - 1], peers[k]) for k in reversed(order)}
    cw = [send(own, own, wsem.at[0], partner)]
    for k in order:
        cg[k].wait_recv()
        part = full.at[core, :, rows(4 - k // 4, 4 - k % 4), :]
        cw.append(send(part, part, wsem.at[k], partner))
    cv.wait_recv()
    for c in cw:
        c.wait_recv()

    basis_steps(scale, dil, full, xall, w, bias, xs)
    mine = xs[tm]
    new_basis[...] = mine
    x = mine.astype(BF16)

    zero = jnp.zeros((K, BLK), BF16)
    pairs = []
    for h in range(2):
        l, r = x[:, 256 * h : 256 * h + BLK], x[:, 256 * h + BLK : 256 * h + 256]
        pairs.append(
            jnp.concatenate(
                [jnp.concatenate([l, zero], axis=1), jnp.concatenate([zero, r], axis=1)], axis=0
            )
        )
    half = obs.shape[0] // 2
    steps = half // S4

    def columns(side, i):
        return pl.ds(pl.multiple_of(side * half + i * S4, S4), S4)

    def product(sl):
        pred = dot(fv[:, sl], x, CONTRACT_FIRST)
        resid = (pred - ov[sl, :].astype(F32)).astype(BF16)
        m = mv[:, sl].astype(F32)
        total = None
        for h in range(2):
            r = dot(pairs[h], resid[:, 256 * h : 256 * h + 256], CONTRACT_LAST)
            t = r[0:K] * m[2 * h : 2 * h + 1] + r[K : 2 * K] * m[2 * h + 1 : 2 * h + 2]
            total = t if total is None else total + t
        return total

    def remote(src, dst, s_sem, r_sem, i, peer):
        return pltpu.make_async_remote_copy(
            src.at[i], dst.at[i], s_sem.at[i], r_sem.at[i], device_id=peer, device_id_type=MESH
        )

    def give_copy(i):
        return remote(give, take, psend, precv, i, partner)

    def code_copy(i):
        return remote(code, got, csend, crecv, i, across)

    def amp_copy(i):
        return remote(amp, gamp, asend, arecv, i, across)

    def final_copy(i):
        sl = columns(core, i)
        return pltpu.make_async_remote_copy(
            out.at[:, sl], out.at[:, sl], fsend.at[i], frecv.at[i], device_id=partner, device_id_type=MESH
        )

    def finish(i):
        code_copy(i).wait_recv()
        amp_copy(i).wait_recv()
        here = code[i].astype(jnp.int32).astype(F32) * amp[i]
        there = got[i].astype(jnp.int32).astype(F32) * gamp[i]
        sl = columns(core, i)
        out[:, sl] = (fv[:, sl].astype(F32) - coef * (here + there)).astype(BF16)
        final_copy(i).start()

    def step(i, carry):
        give[i] = product(columns(1 - core, i))
        give_copy(i).start()
        total = product(columns(core, i))
        give_copy(i).wait_recv()
        total = total + take[i]
        top = jnp.max(jnp.abs(total), axis=0, keepdims=True)
        code[i] = jnp.round(total * (32000.0 / jnp.maximum(top, 1e-30))).astype(jnp.int32).astype(jnp.int16)
        amp[i] = top * (1.0 / 32000.0)
        code_copy(i).start()
        amp_copy(i).start()

        @pl.when(i >= LAG)
        def _():
            finish(i - LAG)

        return carry

    lax.fori_loop(0, steps, step, 0)
    for i in range(steps - LAG, steps):
        finish(i)
    for c in sends:
        c.wait_send()

    def drain(i, carry):
        give_copy(i).wait_send()
        code_copy(i).wait_send()
        amp_copy(i).wait_send()
        final_copy(i).wait_send()
        final_copy(i).wait_recv()
        return carry

    lax.fori_loop(0, steps, drain, 0)


def shards(observed, flags, factors, basis, tcn_weights, tcn_bias, dilations):
    rows, cols = observed.shape
    scale = 1.0 / math.sqrt(rows * lax.axis_size("series"))
    coef = 0.1 / math.sqrt(cols * lax.axis_size("tm"))
    n, m = rows // S1, rows // 2 // S4
    new_basis, new_factors = pl.pallas_call(
        functools.partial(kernel, scale, coef),
        in_specs=[SMEM] + [VMEM] * 3 + [ANY] * 3,
        out_specs=[VMEM, VMEM],
        out_shape=[jax.ShapeDtypeStruct((K, cols), F32), jax.ShapeDtypeStruct((K, rows), BF16)],
        scratch_shapes=[
            pltpu.VMEM((rows, cols), BF16),
            pltpu.VMEM((K, rows), BF16),
            pltpu.VMEM((4, rows), jnp.int32),
            pltpu.VMEM((256, 256), F32),
            pltpu.VMEM((256, K), F32),
            pltpu.VMEM((384, 128), F32),
            pltpu.VMEM((15, 24, 128), F32),
            pltpu.VMEM((24, 128), F32),
            pltpu.VMEM((2, 2, 24, 128), F32),
            pltpu.VMEM((2, 2, 384, 128), F32),
            pltpu.VMEM((2, 2, K, cols), F32),
            pltpu.VMEM((4, K, cols), F32),
            pltpu.VMEM((m, K, S4), F32),
            pltpu.VMEM((m, K, S4), F32),
            pltpu.VMEM((m, K, S4), jnp.int16),
            pltpu.VMEM((m, K, S4), jnp.int16),
            pltpu.VMEM((m, 1, S4), F32),
            pltpu.VMEM((m, 1, S4), F32),
            DMA((n,)),
            DMA((n,)),
            DMA((n,)),
            DMA((51,)),
            DMA((15,)),
            DMA((3,)),
            DMA((15,)),
            DMA((16,)),
            DMA((2,)),
        ]
        + [DMA((m,))] * 8,
        compiler_params=pltpu.CompilerParams(collective_id=0, has_side_effects=True),
        name="step",
    )(dilations, tcn_weights, tcn_bias, basis, flags.T, factors.T, observed)
    return (new_basis, new_factors.T)


def solution(mesh):
    return jax.shard_map(
        shards,
        mesh=mesh,
        in_specs=(
            P("series", "tm"),
            P("series", "tm"),
            P("series", None),
            P(None, "tm"),
            P(),
            P(),
            P(),
        ),
        out_specs=(P(None, "tm"), P("series", None)),
        check_vma=False,
    )
```

```python
import functools
import math

import jax
import jax.numpy as jnp
from jax import lax
from jax.experimental import pallas as pl
from jax.experimental.pallas import tpu as pltpu
from jax.sharding import PartitionSpec as P

K = 64
BLK = 128
ITERS = 3
S1 = 2048
W1 = 3
S4 = 1024
F32 = jnp.float32
BF16 = jnp.bfloat16
MESH = pl.DeviceIdType.MESH
ANY = pl.BlockSpec(memory_space=pl.ANY)
VMEM = pl.BlockSpec(memory_space=pltpu.VMEM)
SMEM = pl.BlockSpec(memory_space=pltpu.SMEM)
DMA = pltpu.SemaphoreType.DMA
CONTRACT_LAST = (((1,), (1,)), ((), ()))
CONTRACT_FIRST = (((0,), (0,)), ((), ()))


def dot(a, b, dims=(((1,), (0,)), ((), ()))):
    return lax.dot_general(a, b, dims, preferred_element_type=F32)


def split(a):
    high = a.astype(BF16)
    return high, (a - high.astype(F32)).astype(BF16)


def basis_steps(scale, dil, full, x_in, w, bias, x_out):
    d0, d1 = dil[0], dil[1]
    tiles = 16
    lane = lax.broadcasted_iota(jnp.int32, (K, BLK), 1)

    def delay(v, d, before):
        rolled = [pltpu.roll(t, d, 1) for t in v]
        return [jnp.where(lane < d, before if j == 0 else rolled[j - 1], rolled[j]) for j in range(tiles)]

    def advance(v, d):
        rolled = [pltpu.roll(t, BLK - d, 1) for t in v]
        zero = jnp.zeros((K, BLK), F32)
        return [
            jnp.where(lane >= BLK - d, zero if j == tiles - 1 else rolled[j + 1], rolled[j])
            for j in range(tiles)
        ]

    def pair(weights, u, v):
        out = []
        for j in range(0, tiles, 2):
            uh, ul = split(jnp.concatenate(u[j : j + 2], axis=1))
            vh, vl = split(jnp.concatenate(v[j : j + 2], axis=1))
            r = dot(weights, jnp.concatenate([uh, vh, ul, vl], axis=0))
            r = r[0:K] + r[K : 2 * K]
            out += [r[:, 0:BLK], r[:, BLK : 2 * BLK]]
        return out

    def packed(a, b):
        ah, al = split(a)
        bh, bl = split(b)
        zero = jnp.zeros((K, 2 * K), BF16)
        top = jnp.concatenate([ah, bh, ah, bh], axis=1)
        low = jnp.concatenate([al, bl, zero], axis=1)
        return jnp.concatenate([top, low], axis=0)

    layer1, layer2 = packed(w[0], w[1]), packed(w[2], w[3])
    back1, back2 = packed(w[0].T, w[1].T), packed(w[2].T, w[3].T)
    eye = lax.broadcasted_iota(jnp.int32, (K, K), 0) == lax.broadcasted_iota(jnp.int32, (K, K), 1)

    def column(i):
        c = jnp.sum(jnp.where(eye, bias[i : i + 1, :], 0.0), axis=1, keepdims=True)
        return jnp.broadcast_to(c, (K, BLK))

    b0, b1 = column(0), column(1)
    start = jnp.maximum(b0, 0.0)
    zero = jnp.zeros((K, BLK), F32)
    grams = []
    for j in range(tiles):
        t, b = j // 4, j % 4
        g = full[t % 2, t // 2, 256 + K * (b // 2) : 320 + K * (b // 2), K * (b % 2) : K * (b % 2) + K]
        gh, gl = split(g)
        rest = g - gh.astype(F32) - gl.astype(F32)
        grams.append(jnp.concatenate([gh, gl, rest.astype(BF16)], axis=0))
    x = [x_in[(j // 4) % 2, j // 8, :, (j % 4) * BLK : (j % 4) * BLK + BLK] for j in range(tiles)]
    for step in range(ITERS):
        z = delay(x, 1, zero)
        a = [v + b0 for v in pair(layer1, delay(z, d0, zero), z)]
        h = [jnp.maximum(v, 0.0) for v in a]
        o = pair(layer2, delay(h, d1, start), h)
        u = [0.1 * (x[j] - z[j] - o[j] - b1) for j in range(tiles)]
        dh = pair(back2, advance(u, d1), u)
        da = [jnp.where(a[j] > 0.0, dh[j], 0.0) for j in range(tiles)]
        dz = pair(back1, advance(da, d0), da)
        dx = advance([u[j] + dz[j] for j in range(tiles)], 1)
        grad = []
        total = zero
        for j in range(tiles):
            t, b = j // 4, j % 4
            r = dot(grams[j], x[j].astype(BF16))
            data = (r[0:K] + (r[K : 2 * K] + r[2 * K : 3 * K])) - full[t % 2, t // 2, b * K : b * K + K, :]
            g = data * scale + (u[j] - dx[j])
            total = total + g * g
            grad.append(g)
        norm = jnp.sqrt(jnp.sum(total, keepdims=True) * (1.0 / (K * BLK * tiles)) + 1e-06)
        x = [x[j] - 0.1 * grad[j] / norm for j in range(tiles)]
    for j in range(tiles):
        x_out[j // 4, :, (j % 4) * BLK : (j % 4) * BLK + BLK] = x[j]


def kernel(
    scale, coef, dil, w_in, bias_in, basis, flg, ft, obs, new_basis, out,
    w, bias, ov, fv, mv, c_acc, g_acc, q, ryz, bx, rx, full, xall, xs, give, take, code, got, amp, gamp,
    so, sf, sm, sw, ssem, yzsem, xsem, gsem, wsem, bsem,
    psend, precv, csend, crecv, asend, arecv, fsend, frecv,
):
    series = lax.axis_index("series")
    tm = lax.axis_index("tm")
    y, z, hi = series // 8, (series // 2) % 4, series % 2
    lo, core = tm // 2, tm % 2

    def at(yy, zz, hh, ll, cc):
        return {"series": (yy % 4) * 8 + (zz % 4) * 2 + hh % 2, "tm": (ll % 2) * 2 + cc % 2}

    order = sorted(range(1, 16), key=lambda k: (min(k // 4, 4 - k // 4) + min(k % 4, 4 - k % 4), k))
    peers = {k: at(y + k // 4, z + k % 4, hi, lo, core) for k in order}
    peers_x = [at(y, z, hi + k // 2, lo + k % 2, core) for k in (1, 2, 3)]
    across = peers_x[0]
    partner = at(y, z, hi, lo, core + 1)

    barrier = pltpu.get_barrier_semaphore()
    for p in [*peers.values(), *peers_x, partner]:
        pl.semaphore_signal(barrier, inc=1, device_id=p, device_id_type=MESH)

    sends = []

    def send(src, dst, sem, peer):
        c = pltpu.make_async_remote_copy(
            src, dst, ssem.at[len(sends)], sem, device_id=peer, device_id_type=MESH
        )
        c.start()
        sends.append(c)
        return c

    n = obs.shape[0] // S1

    def copies(i):
        sl = pl.ds(i * S1, S1)
        return (
            pltpu.make_async_copy(ft.at[:, sl], fv.at[:, sl], sf.at[i]),
            pltpu.make_async_copy(flg.at[:, sl], mv.at[:, sl], sm.at[i]),
            pltpu.make_async_copy(obs.at[sl], ov.at[sl], so.at[i]),
        )

    for i in range(W1):
        for c in copies(i):
            c.start()
    small = (
        pltpu.make_async_copy(basis, xall.at[core, lo], sw.at[0]),
        pltpu.make_async_copy(w_in, w, sw.at[1]),
        pltpu.make_async_copy(bias_in, bias, sw.at[2]),
    )
    for c in small:
        c.start()
    c_acc[...] = jnp.zeros_like(c_acc)
    g_acc[...] = jnp.zeros_like(g_acc)
    for i in range(n):
        for c in copies(i):
            c.wait()
        if i + W1 < n:
            for c in copies(i + W1):
                c.start()
        sl = pl.ds(i * S1, S1)
        f = fv[:, sl]
        m = mv[:, sl].astype(F32).astype(BF16)
        masked = jnp.concatenate([f * m[b : b + 1, :] for b in range(4)], axis=0)
        g_acc[...] += dot(masked, f, CONTRACT_LAST)
        c_acc[0:128] += dot(masked[0:128], ov[sl, 0:256])
        c_acc[128:256] += dot(masked[128:256], ov[sl, 256:512])
        if i == 3:
            pl.semaphore_wait(barrier, 19)
            cb = send(basis, xall.at[core, lo], bsem.at[0], across)
    for b in range(4):
        q[b * K : b * K + K] = c_acc[b * K : b * K + K, (b % 2) * BLK : (b % 2) * BLK + BLK]
    for h in range(2):
        q[256 + K * h : 320 + K * h] = jnp.concatenate(
            [g_acc[128 * h : 128 * h + K], g_acc[128 * h + K : 128 * h + 128]], axis=1
        )

    def rows(dy, dz):
        return pl.ds(96 * ((y + dy) % 4) + 24 * ((z + dz) % 4), 24)

    cq = [send(q.at[rows(k // 4, k % 4)], ryz.at[k - 1], yzsem.at[k - 1], peers[k]) for k in reversed(order)]
    for c in small:
        c.wait()
    cb.wait_recv()
    cv = send(xall.at[core], xall.at[core], bsem.at[1], partner)
    for c in cq:
        c.wait_recv()
    v = [q[rows(0, 0)]] + [ryz[k] for k in range(15)]
    while len(v) > 1:
        v = [v[k] + v[k + 1] for k in range(0, len(v), 2)]
    bx[...] = v[0]
    cx = [send(bx, rx.at[hi, lo], xsem.at[k - 1], peers_x[k - 1]) for k in (1, 2, 3)]
    rx[hi, lo] = v[0]
    for c in cx:
        c.wait_recv()
    row = rows(0, 0)
    full[core, :, row, :] = rx[0] + rx[1]
    own = full.at[core, :, row, :]
    cg = {k: send(own, own, gsem.at[k - 1], peers[k]) for k in reversed(order)}
    cw = [send(own, own, wsem.at[0], partner)]
    for k in order:
        cg[k].wait_recv()
        part = full.at[core, :, rows(4 - k // 4, 4 - k % 4), :]
        cw.append(send(part, part, wsem.at[k], partner))
    cv.wait_recv()
    for c in cw:
        c.wait_recv()

    basis_steps(scale, dil, full, xall, w, bias, xs)
    mine = xs[tm]
    new_basis[...] = mine
    x = mine.astype(BF16)

    zero = jnp.zeros((K, BLK), BF16)
    pairs = []
    for h in range(2):
        l, r = x[:, 256 * h : 256 * h + BLK], x[:, 256 * h + BLK : 256 * h + 256]
        pairs.append(
            jnp.concatenate(
                [jnp.concatenate([l, zero], axis=1), jnp.concatenate([zero, r], axis=1)], axis=0
            )
        )
    half = obs.shape[0] // 2
    steps = half // S4

    def columns(side, i):
        return pl.ds(pl.multiple_of(side * half + i * S4, S4), S4)

    def product(sl):
        pred = dot(fv[:, sl], x, CONTRACT_FIRST)
        resid = (pred - ov[sl, :].astype(F32)).astype(BF16)
        m = mv[:, sl].astype(F32)
        total = None
        for h in range(2):
            r = dot(pairs[h], resid[:, 256 * h : 256 * h + 256], CONTRACT_LAST)
            t = r[0:K] * m[2 * h : 2 * h + 1] + r[K : 2 * K] * m[2 * h + 1 : 2 * h + 2]
            total = t if total is None else total + t
        return total

    def remote(src, dst, s_sem, r_sem, i, peer):
        return pltpu.make_async_remote_copy(
            src.at[i], dst.at[i], s_sem.at[i], r_sem.at[i], device_id=peer, device_id_type=MESH
        )

    def give_copy(i):
        return remote(give, take, psend, precv, i, partner)

    def code_copy(i):
        return remote(code, got, csend, crecv, i, across)

    def amp_copy(i):
        return remote(amp, gamp, asend, arecv, i, across)

    def final_copy(i):
        sl = columns(core, i)
        return pltpu.make_async_remote_copy(
            out.at[:, sl], out.at[:, sl], fsend.at[i], frecv.at[i], device_id=partner, device_id_type=MESH
        )

    def finish(i, carry):
        code_copy(i).wait_recv()
        amp_copy(i).wait_recv()
        here = code[i].astype(jnp.int32).astype(F32) * amp[i]
        there = got[i].astype(jnp.int32).astype(F32) * gamp[i]
        sl = columns(core, i)
        out[:, sl] = (fv[:, sl].astype(F32) - coef * (here + there)).astype(BF16)
        final_copy(i).start()
        return carry

    def step(i, carry):
        give[i] = product(columns(1 - core, i))
        give_copy(i).start()
        total = product(columns(core, i))
        give_copy(i).wait_recv()
        total = total + take[i]
        top = jnp.max(jnp.abs(total), axis=0, keepdims=True)
        code[i] = jnp.round(total * (32000.0 / jnp.maximum(top, 1e-30))).astype(jnp.int32).astype(jnp.int16)
        amp[i] = top * (1.0 / 32000.0)
        code_copy(i).start()
        amp_copy(i).start()
        return carry

    lax.fori_loop(0, steps, step, 0)
    lax.fori_loop(0, steps, finish, 0)
    for c in sends:
        c.wait_send()

    def drain(i, carry):
        give_copy(i).wait_send()
        code_copy(i).wait_send()
        amp_copy(i).wait_send()
        final_copy(i).wait_send()
        final_copy(i).wait_recv()
        return carry

    lax.fori_loop(0, steps, drain, 0)


def shards(observed, flags, factors, basis, tcn_weights, tcn_bias, dilations):
    rows, cols = observed.shape
    scale = 1.0 / math.sqrt(rows * lax.axis_size("series"))
    coef = 0.1 / math.sqrt(cols * lax.axis_size("tm"))
    n, m = rows // S1, rows // 2 // S4
    new_basis, new_factors = pl.pallas_call(
        functools.partial(kernel, scale, coef),
        in_specs=[SMEM] + [ANY] * 6,
        out_specs=[VMEM, VMEM],
        out_shape=[pltpu.VMEM((K, cols), F32), pltpu.VMEM((K, rows), BF16)],
        scratch_shapes=[
            pltpu.VMEM(tcn_weights.shape, F32),
            pltpu.VMEM(tcn_bias.shape, F32),
            pltpu.VMEM((rows, cols), BF16),
            pltpu.VMEM((K, rows), BF16),
            pltpu.VMEM((4, rows), jnp.int32),
            pltpu.VMEM((256, 256), F32),
            pltpu.VMEM((256, K), F32),
            pltpu.VMEM((384, 128), F32),
            pltpu.VMEM((15, 24, 128), F32),
            pltpu.VMEM((24, 128), F32),
            pltpu.VMEM((2, 2, 24, 128), F32),
            pltpu.VMEM((2, 2, 384, 128), F32),
            pltpu.VMEM((2, 2, K, cols), F32),
            pltpu.VMEM((4, K, cols), F32),
            pltpu.VMEM((m, K, S4), F32),
            pltpu.VMEM((m, K, S4), F32),
            pltpu.VMEM((m, K, S4), jnp.int16),
            pltpu.VMEM((m, K, S4), jnp.int16),
            pltpu.VMEM((m, 1, S4), F32),
            pltpu.VMEM((m, 1, S4), F32),
            DMA((n,)),
            DMA((n,)),
            DMA((n,)),
            DMA((3,)),
            DMA((51,)),
            DMA((15,)),
            DMA((3,)),
            DMA((15,)),
            DMA((16,)),
            DMA((2,)),
        ]
        + [DMA((m,))] * 8,
        compiler_params=pltpu.CompilerParams(collective_id=0, has_side_effects=True),
        name="step",
    )(dilations, tcn_weights, tcn_bias, basis, flags.T, factors.T, observed)
    return (new_basis, new_factors.T)


def solution(mesh):
    return jax.shard_map(
        shards,
        mesh=mesh,
        in_specs=(
            P("series", "tm"),
            P("series", "tm"),
            P("series", None),
            P(None, "tm"),
            P(),
            P(),
            P(),
        ),
        out_specs=(P(None, "tm"), P("series", None)),
        check_vma=False,
    )
```

```python
import functools
import math

import jax
import jax.numpy as jnp
from jax import lax
from jax.experimental import pallas as pl
from jax.experimental.pallas import tpu as pltpu
from jax.sharding import PartitionSpec as P

K = 64
BLK = 128
ITERS = 3
S1 = 2048
W1 = 3
S4 = 1024
F32 = jnp.float32
BF16 = jnp.bfloat16
MESH = pl.DeviceIdType.MESH
ANY = pl.BlockSpec(memory_space=pl.ANY)
VMEM = pl.BlockSpec(memory_space=pltpu.VMEM)
SMEM = pl.BlockSpec(memory_space=pltpu.SMEM)
DMA = pltpu.SemaphoreType.DMA
CONTRACT_LAST = (((1,), (1,)), ((), ()))
CONTRACT_FIRST = (((0,), (0,)), ((), ()))


def dot(a, b, dims=(((1,), (0,)), ((), ()))):
    return lax.dot_general(a, b, dims, preferred_element_type=F32)


def split(a):
    high = a.astype(BF16)
    return high, (a - high.astype(F32)).astype(BF16)


TILES = 16


def tile(j):
    return j // 4, slice(None), slice((j % 4) * BLK, (j % 4) * BLK + BLK)


def regularizer(dil, w, bias):
    d0, d1 = dil[0], dil[1]
    tiles = TILES
    lane = lax.broadcasted_iota(jnp.int32, (K, BLK), 1)

    def delay(v, d, before):
        rolled = [pltpu.roll(t, d, 1) for t in v]
        return [jnp.where(lane < d, before if j == 0 else rolled[j - 1], rolled[j]) for j in range(tiles)]

    def advance(v, d):
        rolled = [pltpu.roll(t, BLK - d, 1) for t in v]
        zero = jnp.zeros((K, BLK), F32)
        return [
            jnp.where(lane >= BLK - d, zero if j == tiles - 1 else rolled[j + 1], rolled[j])
            for j in range(tiles)
        ]

    def pair(weights, u, v):
        out = []
        for j in range(0, tiles, 2):
            uh, ul = split(jnp.concatenate(u[j : j + 2], axis=1))
            vh, vl = split(jnp.concatenate(v[j : j + 2], axis=1))
            r = dot(weights, jnp.concatenate([uh, vh, ul, vl], axis=0))
            r = r[0:K] + r[K : 2 * K]
            out += [r[:, 0:BLK], r[:, BLK : 2 * BLK]]
        return out

    def packed(a, b):
        ah, al = split(a)
        bh, bl = split(b)
        zero = jnp.zeros((K, 2 * K), BF16)
        top = jnp.concatenate([ah, bh, ah, bh], axis=1)
        low = jnp.concatenate([al, bl, zero], axis=1)
        return jnp.concatenate([top, low], axis=0)

    layer1, layer2 = packed(w[0], w[1]), packed(w[2], w[3])
    back1, back2 = packed(w[0].T, w[1].T), packed(w[2].T, w[3].T)
    eye = lax.broadcasted_iota(jnp.int32, (K, K), 0) == lax.broadcasted_iota(jnp.int32, (K, K), 1)

    def column(i):
        c = jnp.sum(jnp.where(eye, bias[i : i + 1, :], 0.0), axis=1, keepdims=True)
        return jnp.broadcast_to(c, (K, BLK))

    b0, b1 = column(0), column(1)
    start = jnp.maximum(b0, 0.0)
    zero = jnp.zeros((K, BLK), F32)

    def gradient(x):
        z = delay(x, 1, zero)
        a = [v + b0 for v in pair(layer1, delay(z, d0, zero), z)]
        h = [jnp.maximum(v, 0.0) for v in a]
        o = pair(layer2, delay(h, d1, start), h)
        u = [0.1 * (x[j] - z[j] - o[j] - b1) for j in range(tiles)]
        dh = pair(back2, advance(u, d1), u)
        da = [jnp.where(a[j] > 0.0, dh[j], 0.0) for j in range(tiles)]
        dz = pair(back1, advance(da, d0), da)
        dx = advance([u[j] + dz[j] for j in range(tiles)], 1)
        return [u[j] - dx[j] for j in range(tiles)]

    return gradient


def first_basis(x_in):
    return [x_in[(j // 4) % 2, j // 8, :, (j % 4) * BLK : (j % 4) * BLK + BLK] for j in range(TILES)]


def basis_steps(scale, gradient, full, x_in, x_out):
    grams = []
    for j in range(TILES):
        t, b = j // 4, j % 4
        g = full[t % 2, t // 2, 256 + K * (b // 2) : 320 + K * (b // 2), K * (b % 2) : K * (b % 2) + K]
        gh, gl = split(g)
        rest = g - gh.astype(F32) - gl.astype(F32)
        grams.append(jnp.concatenate([gh, gl, rest.astype(BF16)], axis=0))
    x = first_basis(x_in)
    for step in range(ITERS):
        reg = [x_out[tile(j)] for j in range(TILES)] if step == 0 else gradient(x)
        grad = []
        total = jnp.zeros((K, BLK), F32)
        for j in range(TILES):
            t, b = j // 4, j % 4
            r = dot(grams[j], x[j].astype(BF16))
            data = (r[0:K] + (r[K : 2 * K] + r[2 * K : 3 * K])) - full[t % 2, t // 2, b * K : b * K + K, :]
            g = data * scale + reg[j]
            total = total + g * g
            grad.append(g)
        norm = jnp.sqrt(jnp.sum(total, keepdims=True) * (1.0 / (K * BLK * TILES)) + 1e-06)
        x = [x[j] - 0.1 * grad[j] / norm for j in range(TILES)]
    for j in range(TILES):
        x_out[tile(j)] = x[j]


def kernel(
    scale, coef, dil, w_in, bias_in, basis, flg, ft, obs, new_basis, out,
    w, bias, ov, fv, mv, c_acc, g_acc, q, ryz, bx, rx, full, xall, xs, give, take, code, got, amp, gamp,
    so, sf, sm, sw, ssem, yzsem, xsem, gsem, wsem, bsem,
    psend, precv, csend, crecv, asend, arecv, fsend, frecv,
):
    series = lax.axis_index("series")
    tm = lax.axis_index("tm")
    y, z, hi = series // 8, (series // 2) % 4, series % 2
    lo, core = tm // 2, tm % 2

    def at(yy, zz, hh, ll, cc):
        return {"series": (yy % 4) * 8 + (zz % 4) * 2 + hh % 2, "tm": (ll % 2) * 2 + cc % 2}

    order = sorted(range(1, 16), key=lambda k: (min(k // 4, 4 - k // 4) + min(k % 4, 4 - k % 4), k))
    peers = {k: at(y + k // 4, z + k % 4, hi, lo, core) for k in order}
    peers_x = [at(y, z, hi + k // 2, lo + k % 2, core) for k in (1, 2, 3)]
    across = peers_x[0]
    partner = at(y, z, hi, lo, core + 1)

    barrier = pltpu.get_barrier_semaphore()
    for p in [*peers.values(), *peers_x, partner]:
        pl.semaphore_signal(barrier, inc=1, device_id=p, device_id_type=MESH)

    sends = []

    def send(src, dst, sem, peer):
        c = pltpu.make_async_remote_copy(
            src, dst, ssem.at[len(sends)], sem, device_id=peer, device_id_type=MESH
        )
        c.start()
        sends.append(c)
        return c

    n = obs.shape[0] // S1

    def copies(i):
        sl = pl.ds(i * S1, S1)
        return (
            pltpu.make_async_copy(ft.at[:, sl], fv.at[:, sl], sf.at[i]),
            pltpu.make_async_copy(flg.at[:, sl], mv.at[:, sl], sm.at[i]),
            pltpu.make_async_copy(obs.at[sl], ov.at[sl], so.at[i]),
        )

    for i in range(W1):
        for c in copies(i):
            c.start()
    small = (
        pltpu.make_async_copy(basis, xall.at[core, lo], sw.at[0]),
        pltpu.make_async_copy(w_in, w, sw.at[1]),
        pltpu.make_async_copy(bias_in, bias, sw.at[2]),
    )
    for c in small:
        c.start()
    c_acc[...] = jnp.zeros_like(c_acc)
    g_acc[...] = jnp.zeros_like(g_acc)
    for i in range(n):
        for c in copies(i):
            c.wait()
        if i + W1 < n:
            for c in copies(i + W1):
                c.start()
        sl = pl.ds(i * S1, S1)
        f = fv[:, sl]
        m = mv[:, sl].astype(F32).astype(BF16)
        masked = jnp.concatenate([f * m[b : b + 1, :] for b in range(4)], axis=0)
        g_acc[...] += dot(masked, f, CONTRACT_LAST)
        c_acc[0:128] += dot(masked[0:128], ov[sl, 0:256])
        c_acc[128:256] += dot(masked[128:256], ov[sl, 256:512])
        if i == 3:
            pl.semaphore_wait(barrier, 19)
            cb = send(basis, xall.at[core, lo], bsem.at[0], across)
    for b in range(4):
        q[b * K : b * K + K] = c_acc[b * K : b * K + K, (b % 2) * BLK : (b % 2) * BLK + BLK]
    for h in range(2):
        q[256 + K * h : 320 + K * h] = jnp.concatenate(
            [g_acc[128 * h : 128 * h + K], g_acc[128 * h + K : 128 * h + 128]], axis=1
        )

    def rows(dy, dz):
        return pl.ds(96 * ((y + dy) % 4) + 24 * ((z + dz) % 4), 24)

    cq = [send(q.at[rows(k // 4, k % 4)], ryz.at[k - 1], yzsem.at[k - 1], peers[k]) for k in reversed(order)]
    for c in small:
        c.wait()
    cb.wait_recv()
    cv = send(xall.at[core], xall.at[core], bsem.at[1], partner)
    for c in cq:
        c.wait_recv()
    v = [q[rows(0, 0)]] + [ryz[k] for k in range(15)]
    while len(v) > 1:
        v = [v[k] + v[k + 1] for k in range(0, len(v), 2)]
    bx[...] = v[0]
    cx = [send(bx, rx.at[hi, lo], xsem.at[k - 1], peers_x[k - 1]) for k in (1, 2, 3)]
    rx[hi, lo] = v[0]
    cv.wait_recv()
    gradient = regularizer(dil, w, bias)
    for j, r in enumerate(gradient(first_basis(xall))):
        xs[tile(j)] = r
    for c in cx:
        c.wait_recv()
    row = rows(0, 0)
    full[core, :, row, :] = rx[0] + rx[1]
    own = full.at[core, :, row, :]
    cg = {k: send(own, own, gsem.at[k - 1], peers[k]) for k in reversed(order)}
    cw = [send(own, own, wsem.at[0], partner)]
    for k in order:
        cg[k].wait_recv()
        part = full.at[core, :, rows(4 - k // 4, 4 - k % 4), :]
        cw.append(send(part, part, wsem.at[k], partner))
    for c in cw:
        c.wait_recv()

    basis_steps(scale, gradient, full, xall, xs)
    mine = xs[tm]
    new_basis[...] = mine
    x = mine.astype(BF16)

    zero = jnp.zeros((K, BLK), BF16)
    pairs = []
    for h in range(2):
        l, r = x[:, 256 * h : 256 * h + BLK], x[:, 256 * h + BLK : 256 * h + 256]
        pairs.append(
            jnp.concatenate(
                [jnp.concatenate([l, zero], axis=1), jnp.concatenate([zero, r], axis=1)], axis=0
            )
        )
    half = obs.shape[0] // 2
    steps = half // S4

    def columns(side, i):
        return pl.ds(pl.multiple_of(side * half + i * S4, S4), S4)

    def product(sl):
        pred = dot(fv[:, sl], x, CONTRACT_FIRST)
        resid = (pred - ov[sl, :].astype(F32)).astype(BF16)
        m = mv[:, sl].astype(F32)
        total = None
        for h in range(2):
            r = dot(pairs[h], resid[:, 256 * h : 256 * h + 256], CONTRACT_LAST)
            t = r[0:K] * m[2 * h : 2 * h + 1] + r[K : 2 * K] * m[2 * h + 1 : 2 * h + 2]
            total = t if total is None else total + t
        return total

    def remote(src, dst, s_sem, r_sem, i, peer):
        return pltpu.make_async_remote_copy(
            src.at[i], dst.at[i], s_sem.at[i], r_sem.at[i], device_id=peer, device_id_type=MESH
        )

    def give_copy(i):
        return remote(give, take, psend, precv, i, partner)

    def code_copy(i):
        return remote(code, got, csend, crecv, i, across)

    def amp_copy(i):
        return remote(amp, gamp, asend, arecv, i, across)

    def final_copy(i):
        sl = columns(core, i)
        return pltpu.make_async_remote_copy(
            out.at[:, sl], out.at[:, sl], fsend.at[i], frecv.at[i], device_id=partner, device_id_type=MESH
        )

    def finish(i, carry):
        code_copy(i).wait_recv()
        amp_copy(i).wait_recv()
        here = code[i].astype(jnp.int32).astype(F32) * amp[i]
        there = got[i].astype(jnp.int32).astype(F32) * gamp[i]
        sl = columns(core, i)
        out[:, sl] = (fv[:, sl].astype(F32) - coef * (here + there)).astype(BF16)
        final_copy(i).start()
        return carry

    def step(i, carry):
        give[i] = product(columns(1 - core, i))
        give_copy(i).start()
        total = product(columns(core, i))
        give_copy(i).wait_recv()
        total = total + take[i]
        top = jnp.max(jnp.abs(total), axis=0, keepdims=True)
        code[i] = jnp.round(total * (32000.0 / jnp.maximum(top, 1e-30))).astype(jnp.int32).astype(jnp.int16)
        amp[i] = top * (1.0 / 32000.0)
        code_copy(i).start()
        amp_copy(i).start()
        return carry

    lax.fori_loop(0, steps, step, 0)
    lax.fori_loop(0, steps, finish, 0)
    for c in sends:
        c.wait_send()

    def drain(i, carry):
        give_copy(i).wait_send()
        code_copy(i).wait_send()
        amp_copy(i).wait_send()
        final_copy(i).wait_send()
        final_copy(i).wait_recv()
        return carry

    lax.fori_loop(0, steps, drain, 0)


def shards(observed, flags, factors, basis, tcn_weights, tcn_bias, dilations):
    rows, cols = observed.shape
    scale = 1.0 / math.sqrt(rows * lax.axis_size("series"))
    coef = 0.1 / math.sqrt(cols * lax.axis_size("tm"))
    n, m = rows // S1, rows // 2 // S4
    new_basis, new_factors = pl.pallas_call(
        functools.partial(kernel, scale, coef),
        in_specs=[SMEM] + [ANY] * 6,
        out_specs=[VMEM, VMEM],
        out_shape=[pltpu.VMEM((K, cols), F32), pltpu.VMEM((K, rows), BF16)],
        scratch_shapes=[
            pltpu.VMEM(tcn_weights.shape, F32),
            pltpu.VMEM(tcn_bias.shape, F32),
            pltpu.VMEM((rows, cols), BF16),
            pltpu.VMEM((K, rows), BF16),
            pltpu.VMEM((4, rows), jnp.int32),
            pltpu.VMEM((256, 256), F32),
            pltpu.VMEM((256, K), F32),
            pltpu.VMEM((384, 128), F32),
            pltpu.VMEM((15, 24, 128), F32),
            pltpu.VMEM((24, 128), F32),
            pltpu.VMEM((2, 2, 24, 128), F32),
            pltpu.VMEM((2, 2, 384, 128), F32),
            pltpu.VMEM((2, 2, K, cols), F32),
            pltpu.VMEM((4, K, cols), F32),
            pltpu.VMEM((m, K, S4), F32),
            pltpu.VMEM((m, K, S4), F32),
            pltpu.VMEM((m, K, S4), jnp.int16),
            pltpu.VMEM((m, K, S4), jnp.int16),
            pltpu.VMEM((m, 1, S4), F32),
            pltpu.VMEM((m, 1, S4), F32),
            DMA((n,)),
            DMA((n,)),
            DMA((n,)),
            DMA((3,)),
            DMA((51,)),
            DMA((15,)),
            DMA((3,)),
            DMA((15,)),
            DMA((16,)),
            DMA((2,)),
        ]
        + [DMA((m,))] * 8,
        compiler_params=pltpu.CompilerParams(collective_id=0, has_side_effects=True),
        name="step",
    )(dilations, tcn_weights, tcn_bias, basis, flags.T, factors.T, observed)
    return (new_basis, new_factors.T)


def solution(mesh):
    return jax.shard_map(
        shards,
        mesh=mesh,
        in_specs=(
            P("series", "tm"),
            P("series", "tm"),
            P("series", None),
            P(None, "tm"),
            P(),
            P(),
            P(),
        ),
        out_specs=(P(None, "tm"), P("series", None)),
        check_vma=False,
    )
```
